512 devices in a mesh: space: 32 (over y_lo, z), chaos: 16 (over x, y_hi, core).
Axes of the slice: x: 4, y: 8 (y_hi: 2, y_lo: 4; y = y_hi * 4 + y_lo), z: 8, core: 2. Of those that a mesh axis runs over, the one named last changes fastest.
Arguments:
- load_vectors: bfloat16 [256, 2, 16, 12288], P('chaos', None, None, 'space'), may hold values from -6 to 6
- stiff_tiles: bfloat16 [128, 3, 8, 2, 96, 96], P('space'), may hold values from -0.09375 to 0.09375
- tile_columns: int32 [128, 3], P('space'), may hold values from 0 to 5, as said below
- chaos_index: int32 [8, 256, 32], replicated, may hold values from 0 to 255, as said below
- chaos_value: bfloat16 [8, 256, 32], replicated, may hold values from -1 to 1
Outputs:
- response: float32 [256, 2, 16, 12288], P('chaos', None, None, 'space')
The draws below stay inside these ranges and needn't reach their ends.
Inputs may be any that keep to these rules, and one draw needn't show every extreme that they name: `tile_columns`: in row b of one subdomain with local index l = b % 4, the three numbers are l + 1, one of 0 to l, and one of l + 2 to 5. `chaos_index`: for every k and i the 32 numbers are distinct and the first is i.
All inputs are finite; a program needn't handle non-finite values.
Results may differ from the reference program's by a relative error of at most 0.0029.
Values may be sent and summed in bfloat16 or wider, within the bound.
A program may use at most 128 MiB of HBM per device.

```python
import jax
import jax.numpy as jnp
from jax import lax

TILE = 96
NKL = 8
P_SIZE = 256
NZC = 32
NNZ = 3
BLK_DEV = 4
LOADS = 16
NBLK = 128
NDOF = 12288


def draw_tile_columns(key, part):
    left_key = jax.random.fold_in(key, 11)
    right_key = jax.random.fold_in(key, 12)
    local_row = jnp.arange(NBLK, dtype=jnp.int32) % BLK_DEV
    diagonal = local_row + 1
    left_raw = jax.random.randint(left_key, (NBLK,), 0, 1 << 20, dtype=jnp.int32)
    right_raw = jax.random.randint(right_key, (NBLK,), 0, 1 << 20, dtype=jnp.int32)
    left_col = left_raw % (local_row + 1)
    right_col = local_row + 2 + right_raw % (BLK_DEV - local_row)
    return jnp.stack([diagonal, left_col, right_col], axis=1).astype(jnp.int32)


def draw_chaos_index(key, part):
    score_key = jax.random.fold_in(key, 21)
    raw = jax.random.randint(score_key, (NKL, P_SIZE, P_SIZE), 0, 1 << 20, dtype=jnp.int32)
    columns = jnp.arange(P_SIZE, dtype=jnp.int32)
    scores = raw * P_SIZE + columns[None, None, :]
    diagonal = columns[:, None] == columns[None, :]
    scores = jnp.where(diagonal[None, :, :], jnp.int32(-1), scores)
    top_vals, top_index = lax.top_k(scores, NZC - 1)
    own_terms = jnp.broadcast_to(columns[None, :, None], (NKL, P_SIZE, 1))
    return jnp.concatenate([own_terms, top_index.astype(jnp.int32)], axis=2).astype(jnp.int32)


def shard_levels(stream_key, dims, cuts, least, top_value):
    def one(position, shards_of):
        draws = jax.random.uniform(jax.random.fold_in(jax.random.fold_in(stream_key, 6), position), (shards_of,), jnp.float32, least / len(cuts), top_value / len(cuts))
        return jnp.repeat(jnp.exp(draws), dims[position] // shards_of).reshape((-1,) + (1,) * (len(dims) - position - 1))

    level = one(*cuts[0])
    for cut in cuts[1:]:
        level = level * one(*cut)
    return level


def normal_values(own_key, extent, width, bound, shards=(), kind=jnp.bfloat16):
    entries = width * jax.random.normal(own_key, extent, jnp.float32)
    if shards:
        entries = entries * shard_levels(own_key, extent, shards, -0.22, 0.18)
    return jnp.clip(entries, -bound, bound).astype(kind)


def setup_inputs(seed: int = 0) -> dict:
    seeds = jax.random.split(jax.random.key(seed), 6)
    return {
        "load_vectors": normal_values(seeds[0], (P_SIZE, 2, LOADS, NDOF), 1.0, 6.0, ((0, 16), (3, 32))),
        "stiff_tiles": normal_values(seeds[1], (NBLK, NNZ, NKL, 2, TILE, TILE), (TILE * NNZ * NKL * 2) ** -0.5, 0.09375, ((0, 32),)),
        "tile_columns": draw_tile_columns(jax.random.fold_in(seeds[5], 71), 0),
        "chaos_index": draw_chaos_index(jax.random.fold_in(seeds[5], 71), 0),
        "chaos_value": normal_values(seeds[4], (NKL, P_SIZE, NZC), NZC ** -0.5, 1.0),
    }


def dense_term(index_pair):
    row_index, row_value = index_pair
    columns = jnp.arange(P_SIZE, dtype=jnp.int32)
    matches = row_index[:, :, None] == columns[None, None, :]
    summed = jnp.where(matches, row_value[:, :, None].astype(jnp.float32), jnp.float32(0.0)).sum(axis=1)
    return summed.astype(jnp.bfloat16)


def reference(load_vectors, stiff_tiles, tile_columns, chaos_index, chaos_value):
    coupling = lax.map(dense_term, (chaos_index, chaos_value))
    padded = jnp.pad(load_vectors, ((0, 0), (0, 0), (0, 0), (TILE, TILE)))
    flattened = padded.reshape(P_SIZE, -1)
    rows_all = stiff_tiles.shape[0]
    base = (jnp.arange(rows_all, dtype=jnp.int32) // BLK_DEV) * BLK_DEV
    global_cols = (base[:, None] + tile_columns).astype(jnp.int32)
    start_sum = jnp.zeros((P_SIZE, 2, LOADS, rows_all, TILE), jnp.float32)

    def add_term(kl_term, response):
        mixed = jnp.dot(coupling[kl_term], flattened, preferred_element_type=jnp.float32).astype(jnp.bfloat16)
        mixed = mixed.reshape(P_SIZE, 2, LOADS, rows_all + 2, TILE)
        for tile_slot in range(NNZ):
            columns = jnp.take(mixed, global_cols[:, tile_slot], axis=3).astype(jnp.float32)
            tile_k = stiff_tiles[:, tile_slot, kl_term].astype(jnp.float32)
            real_tile = tile_k[:, 0]
            imag_tile = tile_k[:, 1]
            real_out = jnp.einsum("bxy,prby->prbx", real_tile, columns[:, 0]) - jnp.einsum("bxy,prby->prbx", imag_tile, columns[:, 1])
            imag_out = jnp.einsum("bxy,prby->prbx", real_tile, columns[:, 1]) + jnp.einsum("bxy,prby->prbx", imag_tile, columns[:, 0])
            response = response + jnp.stack([real_out, imag_out], axis=1)
        return response

    response = lax.fori_loop(0, NKL, add_term, start_sum)
    return response.reshape(load_vectors.shape)
```

```python
import functools

import jax
import jax.numpy as jnp
from jax import lax
from jax.experimental import pallas as pl
from jax.experimental.pallas import tpu as pltpu
from jax.sharding import PartitionSpec as P

MESH = pl.DeviceIdType.MESH
TILE = 96
LANE = 128
NKL = 8
NNZ = 3
FAR = (15, 14, 11, 10, 7, 6, 3, 2)
NEAR = (13, 12, 9, 8, 5, 4, 1)
ORDER = FAR + NEAR


def kernel(
    spaces,
    cols,
    xt,
    st,
    ci,
    cv,
    out,
    got,
    left_halo,
    right_halo,
    tiles,
    coup,
    weights,
    xcat,
    mixed,
    result,
    st_sem,
    own_sem,
    in_send,
    in_recv,
    halo_send,
    halo_recv,
    out_send,
    out_recv,
):
    s, c = lax.axis_index("space"), lax.axis_index("chaos")
    has_left, has_right = s > 0, s < spaces - 1
    load_tiles = pltpu.make_async_copy(st, tiles, st_sem)
    load_tiles.start()
    own_in = pltpu.make_async_copy(xt.at[c], got.at[c], own_sem.at[0])
    own_in.start()

    barrier = pltpu.get_barrier_semaphore()
    for k in ORDER:
        pl.semaphore_signal(barrier, inc=1, device_id=(s, c ^ k), device_id_type=MESH)

    @pl.when(has_left)
    def _():
        pl.semaphore_signal(barrier, inc=1, device_id=(s - 1, c), device_id_type=MESH)

    @pl.when(has_right)
    def _():
        pl.semaphore_signal(barrier, inc=1, device_id=(s + 1, c), device_id_type=MESH)

    pl.semaphore_wait(barrier, 15 + has_left.astype(jnp.int32) + has_right.astype(jnp.int32))

    sends = [
        pltpu.make_async_remote_copy(
            xt.at[c ^ k], got.at[c], in_send.at[k], in_recv.at[k], device_id=(s, c ^ k), device_id_type=MESH
        )
        for k in ORDER
    ]
    for copy in sends:
        copy.start()

    def one_coupling(step, _):
        k, half = step // 2, step % 2
        rows = lax.broadcasted_iota(jnp.int32, (LANE, 256), 0) + half * LANE
        total = jnp.zeros((LANE, 256), jnp.float32)
        for n in range(32):
            total = jnp.where(ci[k, n : n + 1, :] == rows, cv[k, n : n + 1, :].astype(jnp.float32), total)
        coup[k, half] = total.T.astype(jnp.bfloat16)
        return 0

    lax.fori_loop(0, 2 * NKL, one_coupling, 0)

    load_tiles.wait()

    def one_weight(step, _):
        b, slot = step // NNZ, step % NNZ
        pad = jnp.zeros((TILE, LANE - TILE), jnp.bfloat16)
        for k in range(NKL):
            real = jnp.concatenate([tiles[b, slot, k, 0], pad], axis=1)
            imag = jnp.concatenate([tiles[b, slot, k, 1], pad], axis=1)
            weights[b, slot, 0:TILE, 2 * k * LANE : (2 * k + 1) * LANE] = real
            weights[b, slot, 0:TILE, (2 * k + 1) * LANE : (2 * k + 2) * LANE] = -imag
            weights[b, slot, TILE : 2 * TILE, 2 * k * LANE : (2 * k + 1) * LANE] = imag
            weights[b, slot, TILE : 2 * TILE, (2 * k + 1) * LANE : (2 * k + 2) * LANE] = real
        return 0

    lax.fori_loop(0, 4 * NNZ, one_weight, 0)

    @pl.when(jnp.logical_not(has_left))
    def _():
        left_halo[...] = jnp.zeros_like(left_halo)

    @pl.when(jnp.logical_not(has_right))
    def _():
        right_halo[...] = jnp.zeros_like(right_halo)

    def to_left(k):
        return pltpu.make_async_remote_copy(
            got.at[c ^ k, :, :, pl.ds(0, LANE)],
            right_halo.at[c ^ k],
            halo_send.at[0, k],
            halo_recv.at[0, k],
            device_id=(s - 1, c),
            device_id_type=MESH,
        )

    def to_right(k):
        return pltpu.make_async_remote_copy(
            got.at[c ^ k, :, :, pl.ds(2 * LANE, LANE)],
            left_halo.at[c ^ k],
            halo_send.at[1, k],
            halo_recv.at[1, k],
            device_id=(s + 1, c),
            device_id_type=MESH,
        )

    def pass_on(k):
        @pl.when(has_left)
        def _():
            to_left(k).start()

        @pl.when(has_right)
        def _():
            to_right(k).start()

    own_in.wait()
    pass_on(0)
    arrivals = {k: copy for k, copy in zip(ORDER, sends)}
    for k in NEAR[::-1] + FAR:
        arrivals[k].wait_recv()
        pass_on(k)

    pad = jnp.zeros((256, LANE - TILE), jnp.bfloat16)
    for part in range(2):
        cells = got[:, part].reshape(256, 3 * LANE)
        for b in range(4):
            block = cells[:, b * TILE : b * TILE + LANE] if b < 3 else jnp.concatenate([cells[:, 3 * TILE :], pad], axis=1)
            xcat[:, (2 * (b + 1) + part) * LANE : (2 * (b + 1) + part + 1) * LANE] = block

    yhi = (c // 2) % 2

    def mix(first, count):
        def one_k(k, _):
            matrix = jnp.concatenate([coup[k, 0], coup[k, 1]], axis=1)
            for g in range(first, first + count):
                value = jnp.dot(matrix, xcat[:, 2 * g * LANE : 2 * (g + 1) * LANE], preferred_element_type=jnp.float32)
                value = value.astype(jnp.bfloat16)
                for q in range(8):
                    place = jnp.where(q % 2 == yhi, 4, 0) + q // 2
                    mixed[g, k, pl.ds(pl.multiple_of(place * 32, 32), 32), :] = value[32 * q : 32 * q + 32]
            return 0

        lax.fori_loop(0, NKL, one_k, 0)

    mix(1, 4)

    @pl.when(has_right)
    def _():
        for k in range(16):
            to_left(k).wait_recv()

    @pl.when(has_left)
    def _():
        for k in range(16):
            to_right(k).wait_recv()

    for part in range(2):
        low = left_halo[:, part].reshape(256, LANE)
        xcat[:, part * LANE : (part + 1) * LANE] = jnp.concatenate([low[:, LANE - TILE :], pad], axis=1)
        xcat[:, (10 + part) * LANE : (11 + part) * LANE] = right_halo[:, part].reshape(256, LANE)
    mix(0, 1)
    mix(5, 1)

    def out_copy(k):
        to = c ^ k
        half = 0 if k & 2 else 1
        place = half * 8 + (to // 4) * 2 + to % 2
        return pltpu.make_async_remote_copy(
            result.at[place], out.at[c], out_send.at[k], out_recv.at[k], device_id=(s, to), device_id_type=MESH
        )

    for half in range(2):
        parts = []
        for b in range(4):
            total = jnp.zeros((128, 2 * TILE), jnp.float32)
            for slot in range(NNZ):
                g = cols[b, slot]
                for k in range(NKL):
                    total = total + lax.dot_general(
                        mixed[g, k, 128 * half : 128 * half + 128, :],
                        weights[b, slot, :, 2 * k * LANE : 2 * (k + 1) * LANE],
                        (((1,), (1,)), ((), ())),
                        preferred_element_type=jnp.float32,
                    )
            parts.append(total)
        for part in range(2):
            value = jnp.concatenate([total[:, part * TILE : (part + 1) * TILE] for total in parts], axis=1)
            result[8 * half : 8 * half + 8, part] = value.astype(jnp.bfloat16).reshape(8, 16, 3 * LANE)
        for k in (NEAR if half else FAR):
            out_copy(k).start()
    own_out = pltpu.make_async_copy(result.at[8 + (c // 4) * 2 + c % 2], out.at[c], own_sem.at[1])
    own_out.start()

    for copy in sends:
        copy.wait_send()

    @pl.when(has_left)
    def _():
        for k in range(16):
            to_left(k).wait_send()

    @pl.when(has_right)
    def _():
        for k in range(16):
            to_right(k).wait_send()

    own_out.wait()
    for k in ORDER:
        out_copy(k).wait()


def body(load_vectors, stiff_tiles, tile_columns, chaos_index, chaos_value):
    spaces = lax.axis_size("space")
    xt = jnp.transpose(load_vectors, (2, 1, 0, 3))
    ci = jnp.transpose(chaos_index, (0, 2, 1))
    cv = jnp.transpose(chaos_value, (0, 2, 1))
    vmem, hbm = pl.BlockSpec(memory_space=pltpu.VMEM), pl.BlockSpec(memory_space=pl.ANY)
    bf16 = jnp.bfloat16
    out = pl.pallas_call(
        functools.partial(kernel, spaces),
        out_shape=jax.ShapeDtypeStruct((16, 2, 16, 384), bf16),
        in_specs=[pl.BlockSpec(memory_space=pltpu.SMEM), hbm, hbm, vmem, vmem],
        out_specs=hbm,
        scratch_shapes=[
            pltpu.VMEM((16, 2, 16, 384), bf16),
            pltpu.VMEM((16, 2, 16, LANE), bf16),
            pltpu.VMEM((16, 2, 16, LANE), bf16),
            pltpu.VMEM(stiff_tiles.shape, bf16),
            pltpu.VMEM((NKL, 2, 256, LANE), bf16),
            pltpu.VMEM((4, NNZ, 2 * TILE, 2 * NKL * LANE), bf16),
            pltpu.VMEM((256, 12 * LANE), bf16),
            pltpu.VMEM((6, NKL, 256, 2 * LANE), bf16),
            pltpu.VMEM((16, 2, 16, 384), bf16),
            pltpu.SemaphoreType.DMA,
            pltpu.SemaphoreType.DMA((2,)),
            pltpu.SemaphoreType.DMA((16,)),
            pltpu.SemaphoreType.DMA((16,)),
            pltpu.SemaphoreType.DMA((2, 16)),
            pltpu.SemaphoreType.DMA((2, 16)),
            pltpu.SemaphoreType.DMA((16,)),
            pltpu.SemaphoreType.DMA((16,)),
        ],
        compiler_params=pltpu.CompilerParams(collective_id=0, has_side_effects=True, vmem_limit_bytes=60 * 1024 * 1024),
    )(tile_columns, xt, stiff_tiles, ci, cv)
    return jnp.transpose(out, (2, 1, 0, 3)).astype(jnp.float32)


def solution(mesh):
    in_specs = (
        P("chaos", None, None, "space"),
        P("space", None, None, None, None, None),
        P("space", None),
        P(),
        P(),
    )
    out_specs = P("chaos", None, None, "space")
    return jax.shard_map(body, mesh=mesh, in_specs=in_specs, out_specs=out_specs, check_vma=False)
```

```python
import functools

import jax
import jax.numpy as jnp
from jax import lax
from jax.experimental import pallas as pl
from jax.experimental.pallas import tpu as pltpu
from jax.sharding import PartitionSpec as P

MESH = pl.DeviceIdType.MESH
TILE = 96
LANE = 128
NKL = 8
NNZ = 3
FAR = (15, 14, 11, 10, 7, 6, 3, 2)
NEAR = (13, 12, 9, 8, 5, 4, 1)
ORDER = FAR + NEAR
PLACES = FAR + NEAR + (0,)
CHUNKS = ((0, 8), (8, 16))


def kernel(
    spaces,
    cols_hbm,
    x,
    st,
    ci_hbm,
    cv_hbm,
    out,
    cols,
    ci,
    cv,
    raw,
    xt,
    got,
    left_halo,
    right_halo,
    tiles,
    coup,
    weights,
    block,
    mixed,
    result,
    back,
    local_sem,
    in_send,
    in_recv,
    halo_send,
    halo_recv,
    out_send,
    out_recv,
):
    s, c = lax.axis_index("space"), lax.axis_index("chaos")
    has_left, has_right = s > 0, s < spaces - 1
    load_x = pltpu.make_async_copy(x, raw, local_sem.at[0])
    load_x.start()
    load_tiles = pltpu.make_async_copy(st, tiles, local_sem.at[1])
    load_terms = [
        pltpu.make_async_copy(ci_hbm, ci, local_sem.at[5]),
        pltpu.make_async_copy(cv_hbm, cv, local_sem.at[6]),
        pltpu.make_async_copy(cols_hbm, cols, local_sem.at[7]),
    ]
    for copy in load_terms:
        copy.start()
    load_tiles.start()

    barrier = pltpu.get_barrier_semaphore()
    for k in ORDER:
        pl.semaphore_signal(barrier, inc=1, device_id=(s, c ^ k), device_id_type=MESH)

    @pl.when(has_left)
    def _():
        pl.semaphore_signal(barrier, inc=1, device_id=(s - 1, c), device_id_type=MESH)

    @pl.when(has_right)
    def _():
        pl.semaphore_signal(barrier, inc=1, device_id=(s + 1, c), device_id_type=MESH)

    load_x.wait()
    for part in range(2):
        for t in range(3):
            value = raw[:, part, :, t * LANE : (t + 1) * LANE]
            xt[t, :, part] = jnp.swapaxes(value, 0, 1)

    pl.semaphore_wait(barrier, 15 + has_left.astype(jnp.int32) + has_right.astype(jnp.int32))

    def in_copy(t, k):
        return pltpu.make_async_remote_copy(
            xt.at[t, c ^ k], got.at[t, c], in_send.at[t, k], in_recv.at[t, k], device_id=(s, c ^ k), device_id_type=MESH
        )

    for t in (0, 2, 1):
        for k in ORDER:
            in_copy(t, k).start()
    own_in = [pltpu.make_async_copy(xt.at[t, c], got.at[t, c], local_sem.at[2 + t]) for t in range(3)]
    for copy in own_in:
        copy.start()

    for copy in load_terms:
        copy.wait()

    def one_coupling(step, _):
        k, half = step // 2, step % 2
        rows = lax.broadcasted_iota(jnp.int32, (LANE, 256), 0) + half * LANE
        total = jnp.zeros((LANE, 256), jnp.float32)
        for n in range(32):
            total = jnp.where(ci[k, n : n + 1, :] == rows, cv[k, n : n + 1, :].astype(jnp.float32), total)
        coup[k, :, pl.ds(pl.multiple_of(half * LANE, LANE), LANE)] = total.T.astype(jnp.bfloat16)
        return 0

    lax.fori_loop(0, 2 * NKL, one_coupling, 0)

    @pl.when(jnp.logical_not(has_left))
    def _():
        left_halo[...] = jnp.zeros_like(left_halo)

    @pl.when(jnp.logical_not(has_right))
    def _():
        right_halo[...] = jnp.zeros_like(right_halo)

    def to_left(k):
        return pltpu.make_async_remote_copy(
            got.at[0, c ^ k],
            right_halo.at[c ^ k],
            halo_send.at[0, k],
            halo_recv.at[0, k],
            device_id=(s - 1, c),
            device_id_type=MESH,
        )

    def to_right(k):
        return pltpu.make_async_remote_copy(
            got.at[2, c ^ k],
            left_halo.at[c ^ k],
            halo_send.at[1, k],
            halo_recv.at[1, k],
            device_id=(s + 1, c),
            device_id_type=MESH,
        )

    def arrived(t, k):
        if k:
            in_copy(t, k).wait_recv()
        else:
            own_in[t].wait()

    ARRIVE = (0,) + NEAR[::-1] + FAR

    load_tiles.wait()

    def one_weight(step, _):
        b, slot = step // NNZ, step % NNZ
        side, below = jnp.zeros((TILE, LANE - TILE), jnp.bfloat16), jnp.zeros((LANE - TILE, 2 * LANE), jnp.bfloat16)
        for k in range(NKL):
            real = jnp.concatenate([tiles[b, slot, k, 0].T, side], axis=1)
            imag = jnp.concatenate([tiles[b, slot, k, 1].T, side], axis=1)
            first, second = 2 * k * LANE, (2 * k + 1) * LANE
            weights[b, slot, first : first + TILE, :] = jnp.concatenate([real, imag], axis=1)
            weights[b, slot, first + TILE : second, :] = below
            weights[b, slot, second : second + TILE, :] = jnp.concatenate([-imag, real], axis=1)
            weights[b, slot, second + TILE : second + LANE, :] = below
        return 0

    lax.fori_loop(0, 4 * NNZ, one_weight, 0)

    for k in ARRIVE:
        arrived(0, k)

        @pl.when(has_left)
        def _():
            to_left(k).start()

    for k in ARRIVE:
        arrived(2, k)

        @pl.when(has_right)
        def _():
            to_right(k).start()

    pad = jnp.zeros((256, LANE - TILE), jnp.bfloat16)

    def tile(t, part):
        return got[t, :, part].reshape(256, LANE)

    def shifted(low, high, start):
        return jnp.concatenate([low[:, start:], high[:, :start]], axis=1)

    def padded(low):
        return jnp.concatenate([low[:, LANE - TILE :], pad], axis=1)

    def mix(g, cells):
        for part in range(2):
            block[:, part * LANE : (part + 1) * LANE] = cells(part)

        def one_k(k, _):
            value = jnp.dot(coup[k], block[...], preferred_element_type=jnp.float32)
            value = value.astype(jnp.bfloat16)
            for q in range(16):
                d = c ^ q
                place = 15 - ((d // 2) % 2 * 8 + d // 4 * 2 + d % 2)
                mixed[g, pl.ds(pl.multiple_of(place * 16, 16), 16), pl.ds(pl.multiple_of(k * 256, 256), 256)] = value[
                    16 * q : 16 * q + 16
                ]
            return 0

        lax.fori_loop(0, NKL, one_k, 0, unroll=True)

    mix(1, lambda part: tile(0, part))
    mix(4, lambda part: padded(tile(2, part)))

    @pl.when(has_right)
    def _():
        for k in range(16):
            to_left(k).wait_recv()

    mix(5, lambda part: right_halo[:, part].reshape(256, LANE))

    @pl.when(has_left)
    def _():
        for k in range(16):
            to_right(k).wait_recv()

    mix(0, lambda part: padded(left_halo[:, part].reshape(256, LANE)))
    for k in ARRIVE:
        arrived(1, k)
    mix(2, lambda part: shifted(tile(0, part), tile(1, part), TILE))
    mix(3, lambda part: shifted(tile(1, part), tile(2, part), 2 * TILE - LANE))

    def out_copy(place):
        k = PLACES[place]
        return pltpu.make_async_remote_copy(
            result.at[place], back.at[c], out_send.at[k], out_recv.at[k], device_id=(s, c ^ k), device_id_type=MESH
        )

    for first, last in CHUNKS:
        rows = (last - first) * 16
        totals = []
        for b in range(4):
            total = jnp.zeros((rows, 2 * LANE), jnp.float32)
            for slot in range(NNZ):
                total = total + jnp.dot(
                    mixed[cols[b, slot], first * 16 : last * 16, :], weights[b, slot], preferred_element_type=jnp.float32
                )
            totals.append(total)
        for part in range(2):
            value = jnp.concatenate([total[:, part * LANE : part * LANE + TILE] for total in totals], axis=1)
            result[first:last, part] = value.astype(jnp.bfloat16).reshape(last - first, 16, 3 * LANE)
        for place in range(first, min(last, 15)):
            out_copy(place).start()
    own_out = pltpu.make_async_copy(result.at[15], back.at[c], local_sem.at[0])
    own_out.start()

    for t in range(3):
        for k in ORDER:
            in_copy(t, k).wait_send()

    @pl.when(has_left)
    def _():
        for k in range(16):
            to_left(k).wait_send()

    @pl.when(has_right)
    def _():
        for k in range(16):
            to_right(k).wait_send()

    own_out.wait()
    for place in range(15):
        out_copy(place).wait()
    for part in range(2):
        for t in range(3):
            value = back[:, part, :, t * LANE : (t + 1) * LANE]
            out[:, part, :, t * LANE : (t + 1) * LANE] = jnp.swapaxes(value, 0, 1)


def body(load_vectors, stiff_tiles, tile_columns, chaos_index, chaos_value):
    spaces = lax.axis_size("space")
    ci = jnp.transpose(chaos_index, (0, 2, 1))
    cv = jnp.transpose(chaos_value, (0, 2, 1))
    hbm = pl.BlockSpec(memory_space=pltpu.HBM)
    bf16 = jnp.bfloat16
    out = pl.pallas_call(
        functools.partial(kernel, spaces),
        out_shape=jax.ShapeDtypeStruct((16, 2, 16, 384), bf16),
        in_specs=[hbm] * 5,
        out_specs=pl.BlockSpec(memory_space=pltpu.VMEM),
        scratch_shapes=[
            pltpu.SMEM(tile_columns.shape, jnp.int32),
            pltpu.VMEM(ci.shape, jnp.int32),
            pltpu.VMEM(cv.shape, bf16),
            pltpu.VMEM((16, 2, 16, 384), bf16),
            pltpu.VMEM((3, 16, 2, 16, LANE), bf16),
            pltpu.VMEM((3, 16, 2, 16, LANE), bf16),
            pltpu.VMEM((16, 2, 16, LANE), bf16),
            pltpu.VMEM((16, 2, 16, LANE), bf16),
            pltpu.VMEM(stiff_tiles.shape, bf16),
            pltpu.VMEM((NKL, 256, 256), bf16),
            pltpu.VMEM((4, NNZ, 2 * NKL * LANE, 2 * LANE), bf16),
            pltpu.VMEM((256, 2 * LANE), bf16),
            pltpu.VMEM((6, 256, 2 * NKL * LANE), bf16),
            pltpu.VMEM((16, 2, 16, 384), bf16),
            pltpu.VMEM((16, 2, 16, 384), bf16),
            pltpu.SemaphoreType.DMA((8,)),
            pltpu.SemaphoreType.DMA((3, 16)),
            pltpu.SemaphoreType.DMA((3, 16)),
            pltpu.SemaphoreType.DMA((2, 16)),
            pltpu.SemaphoreType.DMA((2, 16)),
            pltpu.SemaphoreType.DMA((16,)),
            pltpu.SemaphoreType.DMA((16,)),
        ],
        compiler_params=pltpu.CompilerParams(collective_id=0, has_side_effects=True, vmem_limit_bytes=60 * 1024 * 1024),
    )(tile_columns, load_vectors, stiff_tiles, ci, cv)
    return out.astype(jnp.float32)


def solution(mesh):
    in_specs = (
        P("chaos", None, None, "space"),
        P("space", None, None, None, None, None),
        P("space", None),
        P(),
        P(),
    )
    out_specs = P("chaos", None, None, "space")
    return jax.shard_map(body, mesh=mesh, in_specs=in_specs, out_specs=out_specs, check_vma=False)
```

```python
import functools

import jax
import jax.numpy as jnp
from jax import lax
from jax.experimental import pallas as pl
from jax.experimental.pallas import tpu as pltpu
from jax.sharding import PartitionSpec as P

MESH = pl.DeviceIdType.MESH
TILE = 96
LANE = 128
NKL = 8
NNZ = 3
FAR = (14, 10, 6, 2, 15, 11, 7, 3)
NEAR = (13, 12, 9, 8, 5, 4, 1)
ORDER = FAR + NEAR
PLACES = FAR + NEAR + (0,)
CHUNKS = ((0, 8), (8, 16))


def kernel(
    spaces,
    cols_hbm,
    x,
    st,
    ci_hbm,
    cv_hbm,
    out,
    cols,
    ci,
    cv,
    raw,
    xt,
    got,
    left_halo,
    right_halo,
    tiles,
    coup,
    weights,
    block,
    mixed,
    result,
    back,
    local_sem,
    in_send,
    in_recv,
    halo_send,
    halo_recv,
    out_send,
    out_recv,
):
    s, c = lax.axis_index("space"), lax.axis_index("chaos")
    has_left, has_right = s > 0, s < spaces - 1
    load_x = pltpu.make_async_copy(x, raw, local_sem.at[0])
    load_x.start()
    load_tiles = pltpu.make_async_copy(st, tiles, local_sem.at[1])
    load_terms = [
        pltpu.make_async_copy(ci_hbm, ci, local_sem.at[5]),
        pltpu.make_async_copy(cv_hbm, cv, local_sem.at[6]),
        pltpu.make_async_copy(cols_hbm, cols, local_sem.at[7]),
    ]
    for copy in load_terms:
        copy.start()
    load_tiles.start()

    barrier = pltpu.get_barrier_semaphore()
    for k in ORDER:
        pl.semaphore_signal(barrier, inc=1, device_id=(s, c ^ k), device_id_type=MESH)

    @pl.when(has_left)
    def _():
        pl.semaphore_signal(barrier, inc=1, device_id=(s - 1, c), device_id_type=MESH)

    @pl.when(has_right)
    def _():
        pl.semaphore_signal(barrier, inc=1, device_id=(s + 1, c), device_id_type=MESH)

    load_x.wait()
    for part in range(2):
        for t in range(3):
            value = raw[:, part, :, t * LANE : (t + 1) * LANE]
            xt[t, :, part] = jnp.swapaxes(value, 0, 1)

    pl.semaphore_wait(barrier, 15 + has_left.astype(jnp.int32) + has_right.astype(jnp.int32))

    def in_copy(t, k):
        return pltpu.make_async_remote_copy(
            xt.at[t, c ^ k], got.at[t, c], in_send.at[t, k], in_recv.at[t, k], device_id=(s, c ^ k), device_id_type=MESH
        )

    for t in (0, 2, 1):
        for k in ORDER:
            in_copy(t, k).start()
    own_in = [pltpu.make_async_copy(xt.at[t, c], got.at[t, c], local_sem.at[2 + t]) for t in range(3)]
    for copy in own_in:
        copy.start()

    for copy in load_terms:
        copy.wait()

    def one_coupling(step, _):
        k, half = step // 2, step % 2
        rows = lax.broadcasted_iota(jnp.int32, (LANE, 256), 0) + half * LANE
        total = jnp.zeros((LANE, 256), jnp.float32)
        for n in range(32):
            total = jnp.where(ci[k, n : n + 1, :] == rows, cv[k, n : n + 1, :].astype(jnp.float32), total)
        coup[k, :, pl.ds(pl.multiple_of(half * LANE, LANE), LANE)] = total.T.astype(jnp.bfloat16)
        return 0

    lax.fori_loop(0, 2 * NKL, one_coupling, 0)

    @pl.when(jnp.logical_not(has_left))
    def _():
        left_halo[...] = jnp.zeros_like(left_halo)

    @pl.when(jnp.logical_not(has_right))
    def _():
        right_halo[...] = jnp.zeros_like(right_halo)

    def to_left(k):
        return pltpu.make_async_remote_copy(
            got.at[0, c ^ k],
            right_halo.at[c ^ k],
            halo_send.at[0, k],
            halo_recv.at[0, k],
            device_id=(s - 1, c),
            device_id_type=MESH,
        )

    def to_right(k):
        return pltpu.make_async_remote_copy(
            got.at[2, c ^ k],
            left_halo.at[c ^ k],
            halo_send.at[1, k],
            halo_recv.at[1, k],
            device_id=(s + 1, c),
            device_id_type=MESH,
        )

    def arrived(t, k):
        if k:
            in_copy(t, k).wait_recv()
        else:
            own_in[t].wait()

    ARRIVE = (0,) + NEAR[::-1] + FAR

    load_tiles.wait()

    def one_weight(step, _):
        b, slot = step // NNZ, step % NNZ
        side, below = jnp.zeros((TILE, LANE - TILE), jnp.bfloat16), jnp.zeros((LANE - TILE, 2 * LANE), jnp.bfloat16)
        for k in range(NKL):
            real = jnp.concatenate([tiles[b, slot, k, 0].T, side], axis=1)
            imag = jnp.concatenate([tiles[b, slot, k, 1].T, side], axis=1)
            first, second = 2 * k * LANE, (2 * k + 1) * LANE
            weights[b, slot, first : first + TILE, :] = jnp.concatenate([real, imag], axis=1)
            weights[b, slot, first + TILE : second, :] = below
            weights[b, slot, second : second + TILE, :] = jnp.concatenate([-imag, real], axis=1)
            weights[b, slot, second + TILE : second + LANE, :] = below
        return 0

    lax.fori_loop(0, 4 * NNZ, one_weight, 0)

    for k in ARRIVE:
        arrived(0, k)

        @pl.when(has_left)
        def _():
            to_left(k).start()

    for k in ARRIVE:
        arrived(2, k)

        @pl.when(has_right)
        def _():
            to_right(k).start()

    pad = jnp.zeros((256, LANE - TILE), jnp.bfloat16)

    def tile(t, part):
        return got[t, :, part].reshape(256, LANE)

    def shifted(low, high, start):
        return jnp.concatenate([low[:, start:], high[:, :start]], axis=1)

    def padded(low):
        return jnp.concatenate([low[:, LANE - TILE :], pad], axis=1)

    def mix(g, cells):
        for part in range(2):
            block[:, part * LANE : (part + 1) * LANE] = cells(part)

        def one_k(k, _):
            value = jnp.dot(coup[k], block[...], preferred_element_type=jnp.float32)
            value = value.astype(jnp.bfloat16)
            for q in range(16):
                d = c ^ q
                far = (d // 2) % 2
                place = 15 - (far * 8 + (1 - far) * (d // 4 * 2 + d % 2) + far * (d % 2 * -4 + 4 + d // 4 - (1 - d % 2) * 0))
                mixed[g, pl.ds(pl.multiple_of(place * 16, 16), 16), pl.ds(pl.multiple_of(k * 256, 256), 256)] = value[
                    16 * q : 16 * q + 16
                ]
            return 0

        lax.fori_loop(0, NKL, one_k, 0, unroll=True)

    mix(1, lambda part: tile(0, part))
    mix(4, lambda part: padded(tile(2, part)))

    @pl.when(has_right)
    def _():
        for k in range(16):
            to_left(k).wait_recv()

    mix(5, lambda part: right_halo[:, part].reshape(256, LANE))

    @pl.when(has_left)
    def _():
        for k in range(16):
            to_right(k).wait_recv()

    mix(0, lambda part: padded(left_halo[:, part].reshape(256, LANE)))
    for k in ARRIVE:
        arrived(1, k)
    mix(2, lambda part: shifted(tile(0, part), tile(1, part), TILE))
    mix(3, lambda part: shifted(tile(1, part), tile(2, part), 2 * TILE - LANE))

    def out_copy(place):
        k = PLACES[place]
        return pltpu.make_async_remote_copy(
            result.at[place], back.at[c], out_send.at[k], out_recv.at[k], device_id=(s, c ^ k), device_id_type=MESH
        )

    for first, last in CHUNKS:
        rows = (last - first) * 16
        totals = []
        for b in range(4):
            total = jnp.zeros((rows, 2 * LANE), jnp.float32)
            for slot in range(NNZ):
                total = total + jnp.dot(
                    mixed[cols[b, slot], first * 16 : last * 16, :], weights[b, slot], preferred_element_type=jnp.float32
                )
            totals.append(total)
        for part in range(2):
            value = jnp.concatenate([total[:, part * LANE : part * LANE + TILE] for total in totals], axis=1)
            result[first:last, part] = value.astype(jnp.bfloat16).reshape(last - first, 16, 3 * LANE)
        for place in range(first, min(last, 15)):
            out_copy(place).start()
    own_out = pltpu.make_async_copy(result.at[15], back.at[c], local_sem.at[0])
    own_out.start()

    for t in range(3):
        for k in ORDER:
            in_copy(t, k).wait_send()

    @pl.when(has_left)
    def _():
        for k in range(16):
            to_left(k).wait_send()

    @pl.when(has_right)
    def _():
        for k in range(16):
            to_right(k).wait_send()

    own_out.wait()
    for place in range(15):
        out_copy(place).wait()
    for part in range(2):
        for t in range(3):
            value = back[:, part, :, t * LANE : (t + 1) * LANE]
            out[:, part, :, t * LANE : (t + 1) * LANE] = jnp.swapaxes(value, 0, 1)


def body(load_vectors, stiff_tiles, tile_columns, chaos_index, chaos_value):
    spaces = lax.axis_size("space")
    ci = jnp.transpose(chaos_index, (0, 2, 1))
    cv = jnp.transpose(chaos_value, (0, 2, 1))
    hbm = pl.BlockSpec(memory_space=pltpu.HBM)
    bf16 = jnp.bfloat16
    out = pl.pallas_call(
        functools.partial(kernel, spaces),
        out_shape=jax.ShapeDtypeStruct((16, 2, 16, 384), bf16),
        in_specs=[hbm] * 5,
        out_specs=pl.BlockSpec(memory_space=pltpu.VMEM),
        scratch_shapes=[
            pltpu.SMEM(tile_columns.shape, jnp.int32),
            pltpu.VMEM(ci.shape, jnp.int32),
            pltpu.VMEM(cv.shape, bf16),
            pltpu.VMEM((16, 2, 16, 384), bf16),
            pltpu.VMEM((3, 16, 2, 16, LANE), bf16),
            pltpu.VMEM((3, 16, 2, 16, LANE), bf16),
            pltpu.VMEM((16, 2, 16, LANE), bf16),
            pltpu.VMEM((16, 2, 16, LANE), bf16),
            pltpu.VMEM(stiff_tiles.shape, bf16),
            pltpu.VMEM((NKL, 256, 256), bf16),
            pltpu.VMEM((4, NNZ, 2 * NKL * LANE, 2 * LANE), bf16),
            pltpu.VMEM((256, 2 * LANE), bf16),
            pltpu.VMEM((6, 256, 2 * NKL * LANE), bf16),
            pltpu.VMEM((16, 2, 16, 384), bf16),
            pltpu.VMEM((16, 2, 16, 384), bf16),
            pltpu.SemaphoreType.DMA((8,)),
            pltpu.SemaphoreType.DMA((3, 16)),
            pltpu.SemaphoreType.DMA((3, 16)),
            pltpu.SemaphoreType.DMA((2, 16)),
            pltpu.SemaphoreType.DMA((2, 16)),
            pltpu.SemaphoreType.DMA((16,)),
            pltpu.SemaphoreType.DMA((16,)),
        ],
        compiler_params=pltpu.CompilerParams(collective_id=0, has_side_effects=True, vmem_limit_bytes=60 * 1024 * 1024),
    )(tile_columns, load_vectors, stiff_tiles, ci, cv)
    return out.astype(jnp.float32)


def solution(mesh):
    in_specs = (
        P("chaos", None, None, "space"),
        P("space", None, None, None, None, None),
        P("space", None),
        P(),
        P(),
    )
    out_specs = P("chaos", None, None, "space")
    return jax.shard_map(body, mesh=mesh, in_specs=in_specs, out_specs=out_specs, check_vma=False)
```
